32 devices in a mesh: beam: 2 (over y), chan: 8 (over z, x), tm: 2 (over core).
Axes of the slice: x: 2, y: 2, z: 4, core: 2. Of those that a mesh axis runs over, the one named last changes fastest.
Arguments:
- spectra: float32 [512, 8192], P(('beam', 'chan'), 'tm'), parts along dimension 0, may hold values from -6 to 6
- delay_shifts: int32 [8, 256], replicated, may hold values from 0 to 112, as said below
- box_widths: int32 [20], replicated, may hold values from 1 to 128, as said below
Outputs:
- pulse_power: float32 [512, 8192], P(('beam', 'chan'), 'tm'), parts along dimension 0
The draws below stay inside these ranges and needn't reach their ends.
There are 2 independent parts, one for each index of `beam`. The reference program is written for one: setup_inputs(seed, part) draws one part's arguments, and reference() takes and returns one part's arrays. A program takes and returns all parts, laid end to end along the dimension named above; an argument that names none is the same for every part. Nothing has to cross between parts.
Inputs may be any that keep to these rules, and one draw needn't show every extreme that they name: `delay_shifts`: each section's row of the table contains 112 in some column. `box_widths`: some filter has width 128.
All inputs are finite; a program needn't handle non-finite values.
Results may differ from the reference program's by a relative error of at most 0.000023.
Values sent between devices are 32-bit elements; how exact they have to be, the bound alone decides.
No kernel may reach another device: no remote copies, remote signals or barrier semaphores. Data moves between devices by JAX's collectives and lax.ppermute only.
A program may use at most 64 MiB of HBM per device.

```python
import jax
import jax.numpy as jnp
from jax import lax

LOCAL_SECTIONS = 5
SWAP_SECTIONS = 3
SECTIONS = 8
CHANNELS = 256
TIME_DEV = 4096
TIME = 8192
SHIFT_MAX = 112
WMAX = 128
NBOX = 20
N_CHAN = 8
N_TM = 2


def draw_delay_shifts(key, part):
    drawn = jax.random.randint(jax.random.fold_in(key, 11), (SECTIONS, CHANNELS), 0, SHIFT_MAX + 1, dtype=jnp.int32)
    places = jax.random.randint(jax.random.fold_in(key, 12), (SECTIONS,), 0, CHANNELS, dtype=jnp.int32)
    chosen = jnp.arange(CHANNELS, dtype=jnp.int32)[None, :] == places[:, None]
    return jnp.where(chosen, SHIFT_MAX, drawn).astype(jnp.int32)


def draw_box_widths(key, part):
    drawn = jax.random.randint(jax.random.fold_in(key, 21), (NBOX,), 1, WMAX + 1, dtype=jnp.int32)
    places = jax.random.randint(jax.random.fold_in(key, 22), (), 0, NBOX, dtype=jnp.int32)
    chosen = jnp.arange(NBOX, dtype=jnp.int32) == places
    return jnp.where(chosen, WMAX, drawn).astype(jnp.int32)


def steps_of(key, shape, split, smallest, top_value):
    loudness, own = 1.0, jax.random.fold_in(key, 6)
    for axis_at, shards_of in split:
        draws = jnp.exp(jax.random.uniform(jax.random.fold_in(own, axis_at), (shards_of,), jnp.float32, smallest / len(split), top_value / len(split)))
        loudness = loudness * jnp.repeat(draws, shape[axis_at] // shards_of).reshape([-1 if axis == axis_at else 1 for axis in range(len(shape))])
    return loudness


def gaussian(stream_key, extent, spread, reach, split=(), held_as=jnp.bfloat16):
    values = spread * jax.random.normal(stream_key, extent, jnp.float32)
    if split:
        values = values * steps_of(stream_key, extent, split, -0.22, 0.18)
    return jnp.clip(values, -reach, reach).astype(held_as)


def setup_inputs(seed: int = 0, part: int = 0) -> dict:
    streams_of = jax.random.split(jax.random.key(seed), 4)
    own_keys = jax.random.split(jax.random.fold_in(streams_of[3], part), 4)
    return {
        "spectra": gaussian(own_keys[0], (CHANNELS, TIME), 1.0, 6.0, ((0, 8), (1, 2)), jnp.float32),
        "delay_shifts": draw_delay_shifts(jax.random.fold_in(streams_of[3], 71), part),
        "box_widths": draw_box_widths(jax.random.fold_in(streams_of[3], 71), part),
    }


root_half = 0.7071067811865476


def pair_rows(series, stride):
    total_rows, length = series.shape
    paired = series.reshape(total_rows // (2 * stride), 2, stride, length)
    lower = jnp.broadcast_to(paired[:, 0:1], paired.shape).reshape(total_rows, length)
    upper = jnp.broadcast_to(paired[:, 1:2], paired.shape).reshape(total_rows, length)
    return lower, upper


def delay_add(lower, upper_wide, shifts):
    length = lower.shape[1]

    def take_single(single, shift_by):
        return lax.dynamic_slice_in_dim(single, SHIFT_MAX - shift_by, length)

    delayed = jax.vmap(take_single)(upper_wide, shifts)
    return (lower + delayed) * root_half


def section(series, stride, shifts):
    lower, upper = pair_rows(series, stride)
    upper_wide = jnp.pad(upper, ((0, 0), (SHIFT_MAX, 0)))
    return delay_add(lower, upper_wide, shifts)


def boxcar_power(segment, box_widths):
    length = segment.shape[1] - WMAX
    running = jnp.cumsum(segment, axis=1)
    closing = running[:, WMAX:]

    def add_filter(which, summed):
        span_width = box_widths[which]
        opening = lax.dynamic_slice_in_dim(running, WMAX - span_width, length, 1)
        window_sum = closing - opening
        return summed + window_sum * window_sum / span_width.astype(jnp.float32)

    summed = lax.fori_loop(0, NBOX, add_filter, jnp.zeros(closing.shape, jnp.float32))
    return summed / NBOX


def reference(spectra, delay_shifts, box_widths):
    series = spectra
    for level in range(LOCAL_SECTIONS):
        series = section(series, 2 ** level, delay_shifts[level])
    chan_bits = N_CHAN.bit_length() - 1
    for swap_step in range(SWAP_SECTIONS):
        stride = 2 ** (LOCAL_SECTIONS + chan_bits - SWAP_SECTIONS + swap_step)
        series = section(series, stride, delay_shifts[LOCAL_SECTIONS + swap_step])
    padded = jnp.pad(series, ((0, 0), (WMAX, 0)))
    pieces = []
    for block in range(N_TM):
        segment = padded[:, block * TIME_DEV: block * TIME_DEV + WMAX + TIME_DEV]
        pieces.append(boxcar_power(segment, box_widths))
    return jnp.concatenate(pieces, axis=1)
```

```python
import functools

import jax
import jax.numpy as jnp
from jax import lax
from jax.experimental import pallas as pl
from jax.experimental.pallas import tpu as pltpu
from jax.sharding import PartitionSpec as P

LOCAL_SECTIONS = 5
SWAP_SECTIONS = 3
SECTIONS = LOCAL_SECTIONS + SWAP_SECTIONS
SHIFT_MAX = 112
WMAX = 128
NBOX = 20
LANES = 128
SUB = 8
NBOX_PAD = -(-NBOX // SUB) * SUB


def up_to_lanes(samples):
    return -(-samples // LANES) * LANES


def cols(k):
    return slice(k * LANES, (k + 1) * LANES)


def group_rows(g):
    return slice(g * SUB, (g + 1) * SUB)


def delay_tables(column):
    delay = jnp.broadcast_to(column, (column.shape[0], LANES))
    lane = lax.broadcasted_iota(jnp.int32, delay.shape, 1)
    return (lane - delay) & (LANES - 1), lane < LANES - delay


def shifted(newer, older, tables):
    take, fresh = tables
    mixed = jnp.where(fresh, newer, older)
    return jnp.take_along_axis(mixed, take, axis=1, mode="promise_in_bounds")


def local_kernel(earlier_ref, x_ref, table_ref, *rest):
    groups = x_ref.shape[0] // SUB
    outs, buffers = rest[:groups], rest[groups:]
    head = earlier_ref.shape[1] // LANES
    chunks = head + x_ref.shape[1] // LANES
    dropped = chunks - outs[0].shape[1] // LANES
    sub = lax.broadcasted_iota(jnp.int32, (SUB, LANES), 0)

    def read(level, g, k):
        if level:
            return buffers[(level - 1) % 2][group_rows(g), cols(k)]
        if k < head:
            return earlier_ref[group_rows(g), cols(k)]
        return x_ref[group_rows(g), cols(k - head)]

    for level in range(LOCAL_SECTIONS):
        for g in range(groups):
            tables = delay_tables(table_ref[group_rows(g), level : level + 1])
            older = jnp.zeros((SUB, LANES), jnp.float32)
            for k in range(chunks):
                if 1 << level < SUB:
                    stride = 1 << level
                    own_bit = (sub >> level & 1) == 1
                    own = read(level, g, k)
                    lower = jnp.where(own_bit, pltpu.roll(own, stride, 0), own)
                    upper = jnp.where(own_bit, own, pltpu.roll(own, SUB - stride, 0))
                else:
                    stride = (1 << level) // SUB
                    lower = read(level, g & ~stride, k)
                    upper = read(level, g | stride, k)
                value = lower + shifted(upper, older, tables)
                older = upper
                if level < LOCAL_SECTIONS - 1:
                    buffers[level % 2][group_rows(g), cols(k)] = value
                elif k >= dropped:
                    outs[g][:, cols(k - dropped)] = value


def pair_of(own_ref, partner_ref, upper_own, k):
    own, partner = own_ref[:, cols(k)], partner_ref[:, cols(k)]
    return jnp.where(upper_own, partner, own), jnp.where(upper_own, own, partner)


def bit_mask(table_ref, column):
    return jnp.broadcast_to(table_ref[:, column : column + 1], (SUB, LANES)) == 1


def swap_kernel(delay_columns, bit_column, own_ref, partner_ref, table_ref, *outs):
    dropped = (own_ref.shape[1] - outs[0].shape[1]) // LANES
    upper_own = bit_mask(table_ref, bit_column)
    for column, out_ref in zip(delay_columns, outs):
        tables = delay_tables(table_ref[:, column : column + 1])
        older = None
        for k in range(own_ref.shape[1] // LANES):
            lower, upper = pair_of(own_ref, partner_ref, upper_own, k)
            if k >= dropped:
                out_ref[:, cols(k - dropped)] = lower + shifted(upper, older, tables)
            older = upper


def power_kernel(delay_column, bit_column, own_ref, partner_ref, table_ref, width_ref, weight_ref, out_ref, prefix, suffix, total):
    chunks = out_ref.shape[1] // LANES + 1
    dropped = own_ref.shape[1] // LANES - chunks
    upper_own = bit_mask(table_ref, bit_column)
    tables = delay_tables(table_ref[:, delay_column : delay_column + 1])
    older, pieces = None, []
    for k in range(own_ref.shape[1] // LANES):
        lower, upper = pair_of(own_ref, partner_ref, upper_own, k)
        if k >= dropped:
            pieces.append(lower + shifted(upper, older, tables))
        older = upper
    source = lax.broadcasted_iota(jnp.int32, (LANES, 2 * LANES), 0)
    target = lax.broadcasted_iota(jnp.int32, (LANES, 2 * LANES), 1)
    summing = jnp.where(target < LANES, jnp.where(source <= target, 1.0, 0.0), jnp.where(source > target - LANES, -1.0, 0.0))
    sums = jnp.dot(jnp.concatenate(pieces, axis=0), summing, precision=lax.Precision.HIGHEST, preferred_element_type=jnp.float32)
    prefix[...] = sums[:, :LANES]
    suffix[...] = sums[:, LANES:]
    half = (chunks - 1) // 2

    for start in range(1, chunks, half):
        def add_filter(f, summed):
            width = jnp.broadcast_to(width_ref[pl.ds(f, 1), :], (SUB, LANES))
            weight = jnp.broadcast_to(weight_ref[pl.ds(f, 1), :], (SUB, LANES))
            lane = lax.broadcasted_iota(jnp.int32, (SUB, LANES), 1)
            tables = (lane - width) & (LANES - 1), lane < LANES - width
            updated = []
            for i, value in enumerate(summed):
                k = start + i
                here = prefix[group_rows(k), :]
                window = here - shifted(here, suffix[group_rows(k - 1), :], tables)
                updated.append(value + window * window * weight)
            return tuple(updated)

        zero = jnp.zeros((SUB, LANES), jnp.float32)
        summed = lax.fori_loop(0, NBOX, add_filter, (zero,) * half)
        for i, value in enumerate(summed):
            out_ref[:, cols(start - 1 + i)] = value


VMEM_BLOCK = pl.BlockSpec(memory_space=pltpu.VMEM)


def call(kernel, args, out_lengths, scratch=(), rows=SUB):
    shapes = [jax.ShapeDtypeStruct((rows, length), jnp.float32) for length in out_lengths]
    return pl.pallas_call(
        kernel,
        out_shape=shapes,
        in_specs=[VMEM_BLOCK] * len(args),
        out_specs=[VMEM_BLOCK] * len(shapes),
        scratch_shapes=list(scratch),
        compiler_params=pltpu.CompilerParams(vmem_limit_bytes=8 << 20),
    )(*args)


def swapped(block, flip):
    count = lax.axis_size("chan")
    return lax.ppermute(block, "chan", [(i, i ^ flip) for i in range(count)])


def local(spectra, delay_shifts, box_widths):
    ch_rows, time_len = spectra.shape
    groups = ch_rows // SUB
    steps = lax.axis_size("tm")
    me = lax.axis_index("chan")
    chan_bits = lax.axis_size("chan").bit_length() - 1
    bits = [1 << (chan_bits - SWAP_SECTIONS + i) for i in range(SWAP_SECTIONS)]

    halo = [up_to_lanes((SWAP_SECTIONS - i) * SHIFT_MAX + WMAX) for i in range(SWAP_SECTIONS)] + [WMAX]
    tail = up_to_lanes(SECTIONS * SHIFT_MAX + WMAX)
    earlier = lax.ppermute(spectra[:, -tail:], "tm", [(i, i + 1) for i in range(steps - 1)])

    own_shifts = lax.dynamic_slice_in_dim(delay_shifts, me * ch_rows, ch_rows, 1)
    peer_shifts = lax.dynamic_slice_in_dim(delay_shifts, (me ^ bits[1]) * ch_rows, ch_rows, 1)
    own_bits = jnp.stack([jnp.broadcast_to((me & bit != 0).astype(jnp.int32), (ch_rows,)) for bit in bits])
    table = jnp.concatenate([own_shifts, peer_shifts[LOCAL_SECTIONS + 1 :][:1], own_bits]).T
    widths = jnp.concatenate([box_widths, jnp.full((NBOX_PAD - NBOX,), WMAX, jnp.int32)])
    weights = 1.0 / (widths.astype(jnp.float32) * (NBOX * 2.0**SECTIONS))
    widths = jnp.broadcast_to(widths[:, None], (NBOX_PAD, LANES))
    weights = jnp.broadcast_to(weights[:, None], (NBOX_PAD, LANES))

    wide = pltpu.VMEM((ch_rows, tail + time_len), jnp.float32)
    pieces = call(local_kernel, (earlier, spectra, table), [halo[0] + time_len] * groups, (wide, wide))
    tables = [table[group_rows(g)] for g in range(groups)]
    peers = [swapped(piece, bits[0]) for piece in pieces]
    results = []
    sections = [LOCAL_SECTIONS + i for i in range(SWAP_SECTIONS)]
    for g in range(groups):
        first = functools.partial(swap_kernel, (sections[0],), SECTIONS + 1)
        (one,) = call(first, (pieces[g], peers[g], tables[g]), [halo[1] + time_len])
        one_peer = swapped(one, bits[1])
        second = functools.partial(swap_kernel, (SECTIONS, sections[1]), SECTIONS + 2)
        sent, two = call(second, (one, one_peer, tables[g]), [halo[2] + time_len] * 2)
        two_peer = swapped(sent, bits[1] | bits[2])
        third = functools.partial(power_kernel, sections[2], SECTIONS + 3)
        sums = pltpu.VMEM((SUB * (time_len // LANES + 1), LANES), jnp.float32)
        acc = pltpu.VMEM((SUB, time_len), jnp.float32)
        results += call(third, (two, two_peer, tables[g], widths, weights), [time_len], (sums, sums, acc))
    return jnp.concatenate(results, axis=0)


def solution(mesh):
    in_specs = (P(("beam", "chan"), "tm"), P(), P())
    out_specs = P(("beam", "chan"), "tm")
    return jax.shard_map(local, mesh=mesh, in_specs=in_specs, out_specs=out_specs, check_vma=False)
```

```python
import functools

import jax
import jax.numpy as jnp
from jax import lax
from jax.experimental import pallas as pl
from jax.experimental.pallas import tpu as pltpu
from jax.sharding import PartitionSpec as P


LOCAL_SECTIONS = 5
SWAP_SECTIONS = 3
SECTIONS = LOCAL_SECTIONS + SWAP_SECTIONS
SHIFT_MAX = 112
WMAX = 128
NBOX = 20
LANES = 128
SUB = 8
NBOX_PAD = -(-NBOX // SUB) * SUB
FILTERS_AT_ONCE = 5
OUTPUTS_AT_ONCE = 12

MAIN_LOCAL = -(-LOCAL_SECTIONS * SHIFT_MAX // LANES)
TAIL = -(-(SECTIONS * SHIFT_MAX + WMAX) // LANES)
HEAD = [-(-((SWAP_SECTIONS - i) * SHIFT_MAX + WMAX) // LANES) for i in range(SWAP_SECTIONS + 1)]
MAIN = [MAIN_LOCAL + i for i in range(SWAP_SECTIONS + 2)]


def cols(k):
    return slice(k * LANES, (k + 1) * LANES)


def group_rows(g):
    return slice(g * SUB, (g + 1) * SUB)


def delay_tables(column):
    delay = jnp.broadcast_to(column, (SUB, LANES))
    lane = lax.broadcasted_iota(jnp.int32, (SUB, LANES), 1)
    return (lane - delay) & (LANES - 1), lane < LANES - delay


def shifted(newer, older, tables):
    take, fresh = tables
    mixed = jnp.where(fresh, newer, older)
    return jnp.take_along_axis(mixed, take, axis=1, mode="promise_in_bounds")


def local_sections(groups, table_ref, read_input, buffers, first_input, first_output, end, write):
    sub = lax.broadcasted_iota(jnp.int32, (SUB, LANES), 0)

    def read(level, g, k):
        if level == 0:
            return read_input(g, k)
        return buffers[(level - 1) % 2][group_rows(g), cols(k - first_input)]

    for level in range(LOCAL_SECTIONS):
        first = max(first_input, first_output - (LOCAL_SECTIONS - 1 - level))
        for g in range(groups):
            tables = delay_tables(table_ref[group_rows(g), level : level + 1])

            def pair(k):
                if 1 << level < SUB:
                    stride = 1 << level
                    own_bit = (sub >> level & 1) == 1
                    own = read(level, g, k)
                    lower = jnp.where(own_bit, pltpu.roll(own, stride, 0), own)
                    return lower, jnp.where(own_bit, own, pltpu.roll(own, SUB - stride, 0))
                stride = (1 << level) // SUB
                return read(level, g & ~stride, k), read(level, g | stride, k)

            older = pair(first - 1)[1] if first > first_input else jnp.zeros((SUB, LANES), jnp.float32)
            for k in range(first, end):
                lower, upper = pair(k)
                value = lower + shifted(upper, older, tables)
                older = upper
                if level < LOCAL_SECTIONS - 1:
                    buffers[level % 2][group_rows(g), cols(k - first_input)] = value
                else:
                    write(g, k, value)


def main_local_kernel(x_hbm, table_ref, *rest):
    groups = x_hbm.shape[0] // SUB
    outs, first_ref, (x_ref, *buffers, arrived) = rest[:groups], rest[groups], rest[groups + 1 :]
    copies = [pltpu.make_async_copy(x_hbm.at[group_rows(g), :], x_ref.at[group_rows(g), :], arrived.at[g]) for g in range(groups)]
    for copy in copies:
        copy.start()
    for copy in copies:
        copy.wait()

    def write(g, k, value):
        outs[g][:, cols(k - MAIN[0])] = value

    read = lambda g, k: x_ref[group_rows(g), cols(k)]
    local_sections(groups, table_ref, read, buffers, 0, MAIN[0], x_ref.shape[1] // LANES, write)
    first_ref[...] = x_ref[:, : MAIN[0] * LANES]


def head_local_kernel(earlier_ref, x_ref, table_ref, out_ref, *buffers):
    def read(g, k):
        ref, first = (earlier_ref, -TAIL) if k < 0 else (x_ref, 0)
        return ref[group_rows(g), cols(k - first)]

    def write(g, k, value):
        out_ref[group_rows(g), cols(k + HEAD[0])] = value

    local_sections(x_ref.shape[0] // SUB, table_ref, read, buffers, -TAIL, -HEAD[0], MAIN[0], write)


def bit_mask(table_ref, g, column):
    return jnp.broadcast_to(table_ref[group_rows(g), column : column + 1], (SUB, LANES)) == 1


def readers(section, heads, mains):
    def reader(side):
        def read(g, k):
            if k < MAIN[section]:
                return heads[side][group_rows(g), cols(k + HEAD[section])]
            return mains[side][g][:, cols(k - MAIN[section])]

        return read

    return reader(0), reader(1)


def swap_section(read_own, read_partner, table_ref, g, section, column, first, end, write):
    upper_own = bit_mask(table_ref, g, SECTIONS + section)
    tables = delay_tables(table_ref[group_rows(g), column : column + 1])
    older = None
    for k in range(first - 1, end):
        own, partner = read_own(g, k), read_partner(g, k)
        upper = jnp.where(upper_own, own, partner)
        if k >= first:
            write(g, k, jnp.where(upper_own, partner, own) + shifted(upper, older, tables))
        older = upper


def split_refs(section, groups, has_head, refs):
    heads = refs[:2] if has_head else None
    refs = refs[2 if has_head else 0 :]
    return readers(section, heads, (refs[:groups], refs[groups : 2 * groups])), refs[2 * groups :]


def swap_kernel(section, groups, first, end, *refs):
    has_head = first < MAIN[section]
    (read_own, read_partner), (table_ref, out_ref, *_) = split_refs(section, groups, has_head, refs)

    def write(g, k, value):
        out_ref[group_rows(g), cols(k - first)] = value

    for g in range(groups):
        swap_section(read_own, read_partner, table_ref, g, section, LOCAL_SECTIONS + section, first, end, write)


def power_kernel(section, groups, first, end, *refs):
    has_head = first - 2 < MAIN[section]
    (read_own, read_partner), (table_ref, width_ref, weight_ref, *rest) = split_refs(section, groups, has_head, refs)
    out_ref, prefix, suffix = rest[-3:]
    pieces = {}

    def keep(g, k, value):
        pieces[k, g] = value

    for g in range(groups):
        swap_section(read_own, read_partner, table_ref, g, section, LOCAL_SECTIONS + section, first - 1, end, keep)
    order = sorted(pieces)
    place = {key: i for i, key in enumerate(order)}
    series = jnp.concatenate([pieces[key] for key in order], axis=0)
    source = lax.broadcasted_iota(jnp.int32, (LANES, 2 * LANES), 0)
    target = lax.broadcasted_iota(jnp.int32, (LANES, 2 * LANES), 1)
    summing = jnp.where(target < LANES, jnp.where(source <= target, 1.0, 0.0), jnp.where(source > target - LANES, -1.0, 0.0))
    sums = jnp.dot(series, summing, precision=lax.Precision.HIGHEST, preferred_element_type=jnp.float32)
    prefix[...] = sums[:, :LANES]
    suffix[...] = sums[:, LANES:]
    lane = lax.broadcasted_iota(jnp.int32, (SUB, LANES), 1)
    outputs = [(k, g) for k in range(first, end) for g in range(groups)]

    for start in range(0, len(outputs), OUTPUTS_AT_ONCE):
        block = outputs[start : start + OUTPUTS_AT_ONCE]

        def add_filters(step, summed):
            for i in range(FILTERS_AT_ONCE):
                f = step * FILTERS_AT_ONCE + i
                width = jnp.broadcast_to(width_ref[pl.ds(f, 1), :], (SUB, LANES))
                weight = jnp.broadcast_to(weight_ref[pl.ds(f, 1), :], (SUB, LANES))
                tables = (lane - width) & (LANES - 1), lane < LANES - width
                updated = []
                for (k, g), value in zip(block, summed):
                    here = prefix[group_rows(place[k, g]), :]
                    window = here - shifted(here, suffix[group_rows(place[k - 1, g]), :], tables)
                    updated.append(value + window * window * weight)
                summed = tuple(updated)
            return summed

        zero = jnp.zeros((SUB, LANES), jnp.float32)
        summed = lax.fori_loop(0, NBOX // FILTERS_AT_ONCE, add_filters, (zero,) * len(block))
        for (k, g), value in zip(block, summed):
            out_ref[group_rows(g), cols(k - first)] = value


VMEM_BLOCK = pl.BlockSpec(memory_space=pltpu.VMEM)


class Ordered:
    def __init__(self):
        self.previous = ()

    def __call__(self, kernel, args, out_shapes, scratch=(), spaces=None):
        count, unread = len(args), len(self.previous)

        def body(*refs):
            kernel(*refs[:count], *refs[count + unread :])

        outs = list(pl.pallas_call(
            body,
            out_shape=[jax.ShapeDtypeStruct(shape, jnp.float32) for shape in out_shapes],
            in_specs=(spaces or [VMEM_BLOCK] * count) + [pl.BlockSpec(memory_space=pl.ANY)] * unread,
            out_specs=[VMEM_BLOCK] * len(out_shapes),
            scratch_shapes=[pltpu.VMEM(s, jnp.float32) if isinstance(s, tuple) else s for s in scratch],
            compiler_params=pltpu.CompilerParams(vmem_limit_bytes=8 << 20),
        )(*args, *self.previous))
        self.previous = (outs[0],)
        return outs


def swapped(block, flip):
    count = lax.axis_size("chan")
    return lax.ppermute(block, "chan", [(i, i ^ flip) for i in range(count)])


def local(spectra, delay_shifts, box_widths):
    ch_rows, time_len = spectra.shape
    groups = ch_rows // SUB
    end = time_len // LANES
    steps = lax.axis_size("tm")
    me = lax.axis_index("chan")
    chan_bits = lax.axis_size("chan").bit_length() - 1
    bits = [1 << (chan_bits - SWAP_SECTIONS + i) for i in range(SWAP_SECTIONS)]

    earlier = lax.ppermute(spectra[:, -TAIL * LANES :], "tm", [(i, i + 1) for i in range(steps - 1)])

    own_shifts = lax.dynamic_slice_in_dim(delay_shifts, me * ch_rows, ch_rows, 1)
    own_bits = jnp.stack([jnp.broadcast_to((me & bit != 0).astype(jnp.int32), (ch_rows,)) for bit in bits])
    table = jnp.concatenate([own_shifts, own_bits]).T
    widths = jnp.concatenate([box_widths, jnp.full((NBOX_PAD - NBOX,), WMAX, jnp.int32)])
    weights = 1.0 / (widths.astype(jnp.float32) * (NBOX * 2.0**SECTIONS))
    widths = jnp.broadcast_to(widths[:, None], (NBOX_PAD, LANES))
    weights = jnp.broadcast_to(weights[:, None], (NBOX_PAD, LANES))

    call = Ordered()
    shape = lambda rows, chunks: (rows, chunks * LANES)
    wide = shape(ch_rows, end)
    narrow = shape(ch_rows, TAIL + MAIN[0])
    tables = [table[group_rows(g)] for g in range(groups)]
    filters = (widths, weights)
    cut = MAIN[SWAP_SECTIONS] + 1
    last = SWAP_SECTIONS - 1

    shapes = [shape(SUB, end - MAIN[0])] * groups + [shape(ch_rows, MAIN[0])]
    scratch = (wide, wide, wide, pltpu.SemaphoreType.DMA((groups,)))
    *pieces, first = call(main_local_kernel, (spectra, table), shapes, scratch, [pl.BlockSpec(memory_space=pltpu.HBM), VMEM_BLOCK])
    head = call(head_local_kernel, (earlier, first, table), [shape(ch_rows, HEAD[0] + MAIN[0])], (narrow, narrow))
    mains = [pieces]
    main_peers = [[swapped(piece, bits[0]) for piece in mains[0]]]
    head_peer = [swapped(head[0], bits[0])]

    def main_step(section, g):
        args = (mains[section][g], main_peers[section][g], tables[g])
        if section < last:
            first = MAIN[section + 1]
            (piece,) = call(functools.partial(swap_kernel, section, 1, first, end), args, [shape(SUB, end - first)])
            if g == 0:
                mains.append([])
                main_peers.append([])
            mains[section + 1].append(piece)
            main_peers[section + 1].append(swapped(piece, bits[section + 1]))
        else:
            kernel = functools.partial(power_kernel, section, 1, cut, end)
            results.extend(call(kernel, args + filters, [shape(SUB, end - cut)], [(SUB * (end - cut + 1), LANES)] * 2))

    def head_step(section):
        args = (head[section], head_peer[section], *mains[section], *main_peers[section], table)
        if section < last:
            first, stop = -HEAD[section + 1], MAIN[section + 1]
            head.extend(call(functools.partial(swap_kernel, section, groups, first, stop), args, [shape(ch_rows, stop - first)]))
            head_peer.append(swapped(head[section + 1], bits[section + 1]))
        else:
            kernel = functools.partial(power_kernel, section, groups, 0, cut)
            head.extend(call(kernel, args + filters, [shape(ch_rows, cut)], [(SUB * groups * (cut + 1), LANES)] * 2))

    results = []
    for section, g in work_order(PIECES):
        main_step(section, g) if g < groups else head_step(section)
    return jnp.concatenate([head[-1], jnp.concatenate(results, axis=0)], axis=1)


def work_order(pieces):
    keys = [(g + LAG[section], section, g) for section in range(SWAP_SECTIONS) for g in range(pieces)]
    return [(section, g) for _, section, g in sorted(keys)]


LAG = [0, 1.5, 4.2]
PIECES = 5


def solution(mesh):
    in_specs = (P(("beam", "chan"), "tm"), P(), P())
    out_specs = P(("beam", "chan"), "tm")
    return jax.shard_map(local, mesh=mesh, in_specs=in_specs, out_specs=out_specs, check_vma=False)
```
